32 devices in a mesh: seq: 16 (over z, x, core), tp: 2 (over y).
Axes of the slice: x: 2, y: 2, z: 4, core: 2. Of those that a mesh axis runs over, the one named last changes fastest.
Arguments:
- mixer_input: bfloat16 [8192, 3072], P('seq', 'tp'), may hold values from -6 to 6
- state_write: bfloat16 [8192, 128], P('seq'), may hold values from -2 to 2
- state_read: bfloat16 [8192, 128], P('seq'), may hold values from -2 to 2
- step_size: float32 [8192, 48], P('seq', 'tp'), may hold values from 0.05 to 0.5
- log_decay: float32 [8192, 48], P('seq', 'tp'), may hold values from -1.8 to 0, as said below
- skip_gain: float32 [48], P('tp'), may hold values from 0.5 to 2
- head_gain: float32 [3072], P('tp'), may hold values from 0.25 to 1.75
- mixer_out: bfloat16 [3072, 3072], P('tp'), may hold values from -0.109375 to 0.109375
- residual: bfloat16 [8192, 3072], P('seq', 'tp'), may hold values from -6 to 6
- attn_gain: float32 [3072], replicated, may hold values from 0.25 to 1.75
- qkv_weight: bfloat16 [3072, 3, 1536], P(None, None, 'tp'), may hold values from -2 to 2
Outputs:
- stream: bfloat16 [8192, 3072], P('seq', 'tp')
- attended: bfloat16 [8192, 1536], P('seq', 'tp')
The draws below stay inside these ranges and needn't reach their ends.
Inputs may be any that keep to these rules, and one draw needn't show every extreme that they name: `log_decay`: negative everywhere.
All inputs are finite; a program needn't handle non-finite values.
Results may differ from the reference program's by a relative error of at most 0.03.
Values may be sent and summed in bfloat16 or wider, within the bound.
No kernel may reach another device: no remote copies, remote signals or barrier semaphores. Data moves between devices by JAX's collectives and lax.ppermute only.
A program may use at most 192 MiB of HBM per device.

```python
import math
import jax
import jax.numpy as jnp
from jax import lax

D = 3072
MHEADS = 48
MDIM = 64
STATE = 128
AHEADS = 16
AHD = 96
WINDOW = 2048
TOK_DEV = 512
TOKEN_POSITIONS = 8192
N_TP = 2


def draw_log_decay(key, part):
    random_keys_split = jax.random.split(key, 7)
    slow_share = 0.5
    slow = jax.random.bernoulli(random_keys_split[0], slow_share, (MHEADS,))
    slow_rate = jnp.exp(jax.random.uniform(random_keys_split[1], (MHEADS,), jnp.float32, math.log(0.05), math.log(0.5))) / TOKEN_POSITIONS
    fast_rate = jnp.exp(jax.random.uniform(random_keys_split[2], (MHEADS,), jnp.float32, math.log(1.0 / 50.0), math.log(1.0 / 20.0)))
    head_speed = jnp.where(slow, slow_rate, fast_rate)
    device_multiplier = jnp.repeat(jnp.exp(jax.random.uniform(random_keys_split[3], (TOKEN_POSITIONS // TOK_DEV, MHEADS), jnp.float32, -math.log(2.0), math.log(2.0))), TOK_DEV, axis=0)
    token_multiplier = jnp.exp(jax.random.uniform(random_keys_split[4], (TOKEN_POSITIONS, MHEADS), jnp.float32, -math.log(2.0), math.log(2.0)))
    spike_location = jax.random.randint(random_keys_split[5], (3,), 0, TOKEN_POSITIONS)
    spike_penalty = jax.random.uniform(random_keys_split[6], (3,), jnp.float32, 0.22, 0.51)
    sequence_place = jnp.arange(TOKEN_POSITIONS)
    spike_events = jnp.sum(jnp.where(sequence_place[None, :] == spike_location[:, None], spike_penalty[:, None], 0.0), axis=0)
    return (-(head_speed[None, :] * device_multiplier * token_multiplier + spike_events[:, None])).astype(jnp.float32)


def draw_qkv_weight(key, part):
    random_keys_split = jax.random.split(key, 1)
    embed_all = AHEADS * AHD
    base = jnp.clip(jax.random.normal(random_keys_split[0], (D, 3, embed_all), jnp.float32), -5.0, 5.0) * D ** (-0.5)
    return jnp.clip(base, -2.0, 2.0).astype(jnp.bfloat16)


def block_levels(rng, extent, pieces, smallest, high):
    factor_of, own = 1.0, jax.random.fold_in(rng, 6)
    for position, parts in pieces:
        draws = jnp.exp(jax.random.uniform(jax.random.fold_in(own, position), (parts,), jnp.float32, smallest / len(pieces), high / len(pieces)))
        factor_of = factor_of * jnp.repeat(draws, extent[position] // parts).reshape([-1 if axis == position else 1 for axis in range(len(extent))])
    return factor_of


def noise(rng, shape, deviation, limit, cuts=(), kind=jnp.bfloat16):
    array = deviation * jax.random.normal(rng, shape, jnp.float32)
    if cuts:
        array = array * block_levels(rng, shape, cuts, -0.22, 0.18)
    return jnp.clip(array, -limit, limit).astype(kind)


def setup_inputs(seed: int = 0) -> dict:
    key_list = jax.random.split(jax.random.key(seed), 12)
    return {
        "mixer_input": noise(key_list[0], (TOKEN_POSITIONS, MHEADS * MDIM), 1.0, 6.0, ((0, 16), (1, 2))),
        "state_write": noise(key_list[1], (TOKEN_POSITIONS, STATE), 0.3, 2.0, ((0, 16),)),
        "state_read": noise(key_list[2], (TOKEN_POSITIONS, STATE), 0.3, 2.0, ((0, 16),)),
        "step_size": jnp.clip(jnp.exp(math.log(0.5) - 2.3025851 * jax.random.uniform(key_list[3], (TOKEN_POSITIONS, MHEADS), jnp.float32) ** block_levels(key_list[3], (TOKEN_POSITIONS, MHEADS), ((0, 16), (1, 2)), -0.2, 0.2)), 0.05, 0.5),
        "log_decay": draw_log_decay(jax.random.fold_in(key_list[11], 71), 0),
        "skip_gain": jnp.clip(0.5 + 1.5 * jax.random.uniform(key_list[5], (MHEADS,), jnp.float32) ** block_levels(key_list[5], (MHEADS,), ((0, 2),), -0.2, 0.2), 0.5, 2.0),
        "head_gain": jnp.clip(1.0 + 0.15 * jax.random.normal(key_list[6], (MHEADS * MDIM,), jnp.float32), 0.25, 1.75),
        "mixer_out": noise(key_list[7], (MHEADS * MDIM, D), (MHEADS * MDIM) ** -0.5, 0.109375, ((0, 2),)),
        "residual": noise(key_list[8], (TOKEN_POSITIONS, D), 1.0, 6.0, ((0, 16), (1, 2))),
        "attn_gain": jnp.clip(1.0 + 0.15 * jax.random.normal(key_list[9], (D,), jnp.float32), 0.25, 1.75),
        "qkv_weight": draw_qkv_weight(jax.random.fold_in(key_list[11], 71), 0),
    }


EPSILON = 1e-05

def reference(mixer_input, state_write, state_read, step_size, log_decay, skip_gain, head_gain, mixer_out, residual, attn_gain, qkv_weight):
    span_len = min(TOK_DEV, 256)
    span_count = TOKEN_POSITIONS // span_len

    def blocked(tensor):
        return tensor.reshape((span_count, span_len) + tensor.shape[1:])

    def span_step(carry, blocks):
        inputs, write_rows, read_rows, step_rows, decays = blocks
        cumulative = jnp.cumsum(decays, axis=0)
        totals = cumulative[-1]
        values = inputs.astype(jnp.float32).reshape(span_len, MHEADS, MDIM)
        scaled = (step_rows[:, :, None] * values).astype(jnp.bfloat16)
        intersection = jnp.dot(read_rows, write_rows.T, preferred_element_type=jnp.float32)
        sequence_place = jnp.arange(span_len)
        causal = sequence_place[:, None] >= sequence_place[None, :]
        log_gaps = cumulative.T[:, :, None] - cumulative.T[:, None, :]
        mixing = (jnp.where(causal, jnp.exp(jnp.where(causal, log_gaps, 0.0)), 0.0) * intersection).astype(jnp.bfloat16)
        inner_part = jnp.einsum('hts,shp->thp', mixing.astype(jnp.float32), scaled.astype(jnp.float32))
        carried = jnp.exp(cumulative)[:, :, None] * jnp.einsum('tn,hpn->thp', read_rows.astype(jnp.float32), carry, precision=lax.Precision.HIGHEST)
        outputs = inner_part + carried + skip_gain[None, :, None] * values
        written = jnp.exp(totals[None, :] - cumulative)[:, :, None] * scaled.astype(jnp.float32)
        state_term = jnp.einsum('shp,sn->hpn', written, write_rows.astype(jnp.float32), precision=lax.Precision.HIGHEST)
        new_state = jnp.exp(totals)[:, None, None] * carry + state_term
        return (new_state, outputs)
    initial = jnp.zeros((MHEADS, MDIM, STATE), jnp.float32)
    final_state, outputs = lax.scan(span_step, initial, (blocked(mixer_input), blocked(state_write), blocked(state_read), blocked(step_size), blocked(log_decay)))
    head_outputs = outputs.reshape(TOKEN_POSITIONS, MHEADS, MDIM)
    inverse_rms = lax.rsqrt(lax.optimization_barrier(jnp.mean(head_outputs * head_outputs, axis=2, keepdims=True)) + EPSILON)
    normed = ((head_outputs * inverse_rms).reshape(TOKEN_POSITIONS, MHEADS * MDIM) * head_gain).astype(jnp.bfloat16)
    run_len = MHEADS * MDIM // N_TP
    total_sum = residual.astype(jnp.float32)
    for group_index in range(N_TP):
        partial_value = jnp.dot(normed[:, group_index * run_len:(group_index + 1) * run_len], mixer_out[group_index * run_len:(group_index + 1) * run_len], preferred_element_type=jnp.float32)
        total_sum = total_sum + lax.optimization_barrier(partial_value.astype(jnp.bfloat16)).astype(jnp.float32)
    stream = total_sum.astype(jnp.bfloat16)
    stream_wide = stream.astype(jnp.float32)
    normed_stream = (stream_wide * lax.rsqrt(lax.optimization_barrier(jnp.mean(stream_wide * stream_wide, axis=1, keepdims=True)) + EPSILON) * attn_gain).astype(jnp.bfloat16)
    embed_all = AHEADS * AHD
    projected = jnp.dot(normed_stream, qkv_weight.reshape(D, 3 * embed_all), preferred_element_type=jnp.float32).astype(jnp.bfloat16).reshape(TOKEN_POSITIONS, 3, embed_all)
    query_all = projected[:, 0].reshape(TOKEN_POSITIONS, AHEADS, AHD)
    padding = jnp.zeros((WINDOW, AHEADS, AHD), jnp.bfloat16)
    padded_keys = jnp.concatenate([padding, projected[:, 1].reshape(TOKEN_POSITIONS, AHEADS, AHD)], axis=0)
    padded_values = jnp.concatenate([padding, projected[:, 2].reshape(TOKEN_POSITIONS, AHEADS, AHD)], axis=0)

    def one_block(block_index):
        row_start = (block_index * TOK_DEV).astype(jnp.int32)
        queries = lax.dynamic_slice_in_dim(query_all, row_start, TOK_DEV, 0)
        key_part = lax.dynamic_slice_in_dim(padded_keys, row_start, TOK_DEV + WINDOW, 0)
        value_part = lax.dynamic_slice_in_dim(padded_values, row_start, TOK_DEV + WINDOW, 0)
        scores = jnp.einsum('thd,rhd->htr', queries.astype(jnp.float32), key_part.astype(jnp.float32)) * AHD ** (-0.5)
        query_pos = jnp.arange(TOK_DEV)
        key_pos = jnp.arange(TOK_DEV + WINDOW)
        first_valid = WINDOW - row_start
        allowed = (key_pos[None, :] > query_pos[:, None]) & (key_pos[None, :] <= query_pos[:, None] + WINDOW) & (key_pos[None, :] >= first_valid)
        masked = jnp.where(allowed[None], scores, -jnp.inf)
        peak = lax.optimization_barrier(jnp.max(masked, axis=2, keepdims=True))
        raised = jnp.exp(masked - peak)
        weights = (raised / lax.optimization_barrier(jnp.sum(raised, axis=2, keepdims=True))).astype(jnp.bfloat16)
        result = jnp.einsum('htr,rhd->thd', weights.astype(jnp.float32), value_part.astype(jnp.float32))
        return result.astype(jnp.bfloat16).reshape(TOK_DEV, embed_all)
    blocks_out = lax.map(one_block, jnp.arange(TOKEN_POSITIONS // TOK_DEV, dtype=jnp.int32))
    attended = blocks_out.reshape(TOKEN_POSITIONS, embed_all)
    return (stream, attended)
```

```python
import math

import jax
import jax.numpy as jnp
from jax import lax
from jax.experimental import pallas as pl
from jax.experimental.pallas import tpu as pltpu
from jax.sharding import PartitionSpec as P


AHD = 96
EPSILON = 1e-05
CHUNKS = (1, 1, 1, 1)
LOCAL = (3, 2, 1)


def attend(query, blocks, valid, head_dim):
    length, width = query.shape
    group = math.lcm(head_dim, 128)
    heads = group // head_dim
    groups = width // group
    pieces = [len(b) for b in blocks]
    flat = [p for b in blocks for p in b]
    n_full = len(blocks) - 2
    scale = head_dim ** (-0.5)

    def kernel(valid_ref, q_ref, *refs):
        k_refs, v_refs, at = [], [], 0
        for count in pieces:
            k_refs.append(refs[2 * at : 2 * (at + count) : 2])
            v_refs.append(refs[2 * at + 1 : 2 * (at + count) : 2])
            at += count
        o_ref, s_ref = refs[2 * at], refs[2 * at + 1]
        row = lax.broadcasted_iota(jnp.int32, (length, length), 0)
        col = lax.broadcasted_iota(jnp.int32, (length, length), 1)
        near = col <= row
        flags = [valid_ref[i] > 0 for i in range(1 + n_full)]
        far_bias = jnp.where(flags[0], 0.0, -jnp.inf)
        outs = {}
        for j in range(heads):
            lo = j * head_dim // 128 * 128
            hi = -(-(j + 1) * head_dim // 128) * 128
            lane = lo + lax.broadcasted_iota(jnp.int32, (length, hi - lo), 1)
            mine = (lane >= j * head_dim) & (lane < (j + 1) * head_dim)
            q = jnp.where(mine, q_ref[:, lo:hi], jnp.zeros((), q_ref.dtype))

            def load(refs):
                return jnp.concatenate([r[:, lo:hi] for r in refs], axis=0)

            def score(refs):
                return lax.dot_general(
                    q, load(refs), (((1,), (1,)), ((), ())), preferred_element_type=jnp.float32
                )

            def rowmax(s):
                return jnp.max(s, axis=1, keepdims=True)

            s = jnp.where(near, score(k_refs[-1]), score(k_refs[0]) + far_bias)
            s_ref[0] = s
            peak = rowmax(s)
            for i in range(n_full):
                s = score(k_refs[1 + i])
                s_ref[1 + i] = s
                peak = jnp.maximum(peak, jnp.where(flags[1 + i], rowmax(s), -jnp.inf))
            peak = peak * scale
            p = jnp.exp(s_ref[0] * scale - peak)
            total = jnp.sum(p, axis=1, keepdims=True)
            p = p.astype(jnp.bfloat16)
            zero = jnp.zeros_like(p)
            acc = jnp.dot(
                jnp.where(near, p, zero), load(v_refs[-1]), preferred_element_type=jnp.float32
            )
            acc += jnp.dot(
                jnp.where(near, zero, p), load(v_refs[0]), preferred_element_type=jnp.float32
            )
            for i in range(n_full):
                p = jnp.exp(s_ref[1 + i] * scale - jnp.where(flags[1 + i], peak, jnp.inf))
                total += jnp.sum(p, axis=1, keepdims=True)
                acc += jnp.dot(
                    p.astype(jnp.bfloat16), load(v_refs[1 + i]), preferred_element_type=jnp.float32
                )
            acc = acc * (1.0 / total)
            for t in range(lo, hi, 128):
                piece = jnp.where(mine[:, t - lo : t - lo + 128], acc[:, t - lo : t - lo + 128], 0.0)
                outs[t] = outs[t] + piece if t in outs else piece
        for t, piece in outs.items():
            o_ref[:, t : t + 128] = piece.astype(o_ref.dtype)

    specs = [
        pl.BlockSpec(memory_space=pltpu.SMEM),
        pl.BlockSpec((length, group), lambda g: (0, g)),
    ]
    args = [valid, query]
    for p in flat:
        specs.append(pl.BlockSpec((p.shape[0], group), lambda g: (0, g)))
        specs.append(pl.BlockSpec((p.shape[0], group), lambda g: (0, g + groups)))
        args += [p, p]
    keys = len(blocks) * length
    return pl.pallas_call(
        kernel,
        grid=(groups,),
        in_specs=specs,
        out_specs=pl.BlockSpec((length, group), lambda g: (0, g)),
        out_shape=jax.ShapeDtypeStruct((length, width), query.dtype),
        scratch_shapes=[pltpu.VMEM((1 + n_full, length, length), jnp.float32)],
        cost_estimate=pl.CostEstimate(
            flops=4 * length * keys * width,
            transcendentals=length * keys * width // head_dim,
            bytes_accessed=2 * (len(blocks) * 2 + 2) * length * width,
        ),
        compiler_params=pltpu.CompilerParams(vmem_limit_bytes=31 << 20),
        name="attend",
    )(*args)


def stream_and_project(own, got, residual, far_residual, side, gain, weight, at, buffers):
    rows, width = own.shape
    length, half = residual.shape
    parts, _, embed = weight.shape
    tile = embed // 2
    steps = embed // tile
    index = at // rows

    def kernel(side_ref, own_ref, got_ref, res_ref, far_ref, gain_ref, w_ref, *refs):
        stream_ref, n_ref, kv_ref, w_sum = refs[len(buffers) :]
        first = side_ref[0] == 0

        @pl.when(pl.program_id(0) == 0)
        def _():
            squares = jnp.zeros((rows, 1), jnp.float32)
            kept = []
            for h in range(2):
                lanes = slice(h * half, (h + 1) * half)
                base = jnp.where(first == (h == 0), res_ref[...], far_ref[...])
                wide = base.astype(jnp.float32) + (
                    own_ref[:, lanes].astype(jnp.float32) + got_ref[:, lanes].astype(jnp.float32)
                )
                stream = wide.astype(own_ref.dtype)
                kept.append(stream)
                wide = stream.astype(jnp.float32)
                w_sum[:, lanes] = wide
                squares += jnp.sum(wide * wide, axis=1, keepdims=True)
            stream_ref[...] = jnp.where(first, kept[0], kept[1])
            inverse = lax.rsqrt(squares / width + EPSILON)
            n_ref[...] = (w_sum[...] * inverse * gain_ref[...]).astype(n_ref.dtype)

        kv_ref[...] = jnp.dot(n_ref[...], w_ref[0], preferred_element_type=jnp.float32).astype(
            kv_ref.dtype
        )

    flat = lambda a: pl.BlockSpec(a.shape, lambda i: (0, 0))
    return pl.pallas_call(
        kernel,
        grid=((parts - 1) * steps,),
        in_specs=[
            pl.BlockSpec(memory_space=pltpu.SMEM),
            flat(own),
            flat(got),
            pl.BlockSpec((rows, half), lambda i: (index, 0)),
            pl.BlockSpec((rows, half), lambda i: (index, 0)),
            flat(gain),
            pl.BlockSpec((1, width, tile), lambda i: (1 + i // steps, 0, i % steps)),
        ]
        + [pl.BlockSpec(memory_space=pl.ANY)] * len(buffers),
        out_specs=[
            pl.BlockSpec((rows, half), lambda i: (index, 0)),
            pl.BlockSpec((rows, width), lambda i: (index, 0)),
            pl.BlockSpec((rows, tile), lambda i: (0, i)),
        ],
        out_shape=[
            jax.ShapeDtypeStruct((length, half), own.dtype),
            jax.ShapeDtypeStruct((length, width), own.dtype),
            pltpu.HBM((rows, (parts - 1) * embed), own.dtype),
        ],
        scratch_shapes=[pltpu.VMEM((rows, width), jnp.float32)],
        input_output_aliases={7 + i: i for i in range(len(buffers))},
        cost_estimate=pl.CostEstimate(
            flops=2 * rows * width * (parts - 1) * embed,
            transcendentals=rows,
            bytes_accessed=2 * width * (parts - 1) * embed,
        ),
        compiler_params=pltpu.CompilerParams(vmem_limit_bytes=17 << 20),
        name="stream_and_project",
    )(side, *held(own), got, *held(residual, far_residual, gain), weight, *buffers)


def project_queries(normed_stream, weight):
    length, width = normed_stream.shape
    embed = weight.shape[2]
    tile = embed // 3

    def kernel(n_ref, w_ref, q_ref):
        q_ref[...] = jnp.dot(n_ref[...], w_ref[0], preferred_element_type=jnp.float32).astype(
            q_ref.dtype
        )

    return pl.pallas_call(
        kernel,
        grid=(embed // tile,),
        in_specs=[
            pl.BlockSpec((length, width), lambda i: (0, 0)),
            pl.BlockSpec((1, width, tile), lambda i: (0, 0, i)),
        ],
        out_specs=pl.BlockSpec((length, tile), lambda i: (0, i)),
        out_shape=jax.ShapeDtypeStruct((length, embed), normed_stream.dtype),
        cost_estimate=pl.CostEstimate(
            flops=2 * length * width * embed,
            transcendentals=0,
            bytes_accessed=2 * width * (embed + length),
        ),
        compiler_params=pltpu.CompilerParams(vmem_limit_bytes=14 << 20),
        name="project_queries",
    )(normed_stream, weight)


def held(*arrays):
    return [pltpu.with_memory_space_constraint(a, pltpu.HBM) for a in arrays]


def log2(n):
    return n.bit_length() - 1


def expander(first, kind, group, head_dim, slots):
    row = lax.broadcasted_iota(jnp.int32, (128, group), 0)
    lane = lax.broadcasted_iota(jnp.int32, (128, group), 1)
    gap = row - (kind * 2 * slots + first) - lax.shift_right_logical(lane, log2(head_dim))
    return ((gap == 0) | (gap == slots)).astype(jnp.bfloat16)


def terms(a):
    high = a.astype(jnp.bfloat16).astype(jnp.float32)
    return [high, a - high]


def write_states(inputs, step_rows, decay_rows, write_rows, head_dim, slots, heads, spans):
    length, channels = inputs.shape
    head_count = step_rows.shape[0]
    size = write_rows.shape[1]
    span = length // spans
    group = heads * head_dim

    def kernel(x_ref, p_ref, d_ref, b_ref, o_ref, steps_ref, fades_ref, carries_ref, gaps_ref, rows_ref):
        i = pl.program_id(0)

        @pl.when(i == 0)
        def _():
            before = lax.broadcasted_iota(jnp.int32, (span, span), 0)
            after = lax.broadcasted_iota(jnp.int32, (span, span), 1)
            ones = (before <= after).astype(jnp.float32)
            start = jnp.zeros((head_count, 1), jnp.float32)
            grown, overall, ends = [], [], []
            for s in range(spans):
                part = jnp.dot(
                    d_ref[:, s * span : (s + 1) * span],
                    ones,
                    preferred_element_type=jnp.float32,
                    precision=lax.Precision.HIGHEST,
                )
                last = part[:, span - 1 :]
                grown.append(part)
                overall.append(part + start)
                ends.append(jnp.broadcast_to(last, (head_count, span)))
                start = start + last
            grown, overall, ends = (jnp.concatenate(a, axis=1) for a in (grown, overall, ends))
            rows_ref[...] = grown
            pad = jnp.zeros((slots - head_count, length), jnp.float32)

            def columns(parts):
                stacked = [a for part in parts for a in (part, pad)]
                rest = 128 - slots * len(parts)
                if rest:
                    stacked.append(jnp.zeros((rest, length), jnp.float32))
                return jnp.concatenate(stacked, axis=0).T

            step = p_ref[...]
            steps_ref[...] = columns(terms(step * jnp.exp(start - overall)) + terms(step)).astype(
                jnp.bfloat16
            )
            fades_ref[...] = columns(terms(jnp.exp(grown)) + terms(jnp.exp(ends - grown))).astype(
                jnp.bfloat16
            )
            carries_ref[...] = columns(terms(jnp.exp(overall))).astype(jnp.bfloat16)
            gaps_ref[...] = columns([grown])
            decay = jnp.broadcast_to(jnp.exp(start), (head_count, size))
            o_ref[channels:, :] = jnp.concatenate(terms(decay), axis=0).astype(jnp.bfloat16)

        spread = expander(i * heads, 0, group, head_dim, slots)
        weight = jnp.dot(steps_ref[...], spread, preferred_element_type=jnp.float32)
        u = (x_ref[...].astype(jnp.float32) * weight).astype(jnp.bfloat16)
        o_ref[pl.ds(pl.multiple_of(i * group, group), group), :] = lax.dot_general(
            u, b_ref[...], (((0,), (0,)), ((), ())), preferred_element_type=jnp.float32
        ).astype(o_ref.dtype)

    full = lambda a: pl.BlockSpec(a.shape, lambda i: (0, 0))
    shapes = [
        pltpu.HBM((channels + 2 * head_count, size), jnp.bfloat16),
        pltpu.HBM((length, 128), jnp.bfloat16),
        pltpu.HBM((length, 128), jnp.bfloat16),
        pltpu.HBM((length, 128), jnp.bfloat16),
        pltpu.HBM((length, 128), jnp.float32),
        pltpu.HBM((head_count, length), jnp.float32),
    ]
    return pl.pallas_call(
        kernel,
        grid=(channels // group,),
        in_specs=[
            pl.BlockSpec((length, group), lambda i: (0, i)),
            full(step_rows),
            full(decay_rows),
            full(write_rows),
        ],
        out_specs=[full(a) for a in shapes],
        out_shape=shapes,
        cost_estimate=pl.CostEstimate(
            flops=2 * length * channels * size,
            transcendentals=0,
            bytes_accessed=2 * (length + size) * channels,
        ),
        compiler_params=pltpu.CompilerParams(vmem_limit_bytes=14 << 20),
        name="write_states",
    )(*held(inputs, step_rows, decay_rows, write_rows))


def local_outputs(
    inputs, steps, fades, grown, rows, write_rows, read_rows, skip, head_dim, slots, heads, spans,
    offset, count, buffers,
):
    length, channels = inputs.shape
    span = length // spans
    wide = 2 * head_dim
    group = heads * head_dim

    def kernel(x_ref, p_ref, f_ref, t_ref, g_ref, b_ref, c_ref, k_ref, *refs):
        o_ref, i_ref = refs[len(buffers) :]
        first = (pl.program_id(0) + offset) * heads

        @pl.when(pl.program_id(0) == 0)
        def _():
            for s in range(spans):
                at = s * span
                inner = lax.dot_general(
                    c_ref[at : at + span, :],
                    b_ref[at : at + span, :],
                    (((1,), (1,)), ((), ())),
                    preferred_element_type=jnp.float32,
                )
                row = lax.broadcasted_iota(jnp.int32, (span, span), 0)
                col = lax.broadcasted_iota(jnp.int32, (span, span), 1)
                i_ref[s] = jnp.where(row >= col, inner, 0.0)

        columns = pltpu.roll(t_ref[...], lax.rem(t_ref.shape[1] - first, t_ref.shape[1]), 1)
        step = jnp.dot(
            p_ref[...],
            expander(first, 1, group, head_dim, slots),
            preferred_element_type=jnp.float32,
        )
        grow = jnp.dot(
            f_ref[...],
            expander(first, 0, group, head_dim, slots),
            preferred_element_type=jnp.float32,
        )
        fade = jnp.dot(
            f_ref[...],
            expander(first, 1, group, head_dim, slots),
            preferred_element_type=jnp.float32,
        )
        lane = lax.broadcasted_iota(jnp.int32, (span, wide), 1)
        for pair in range(heads // 2):
            at = slice(pair * wide, (pair + 1) * wide)
            state = None
            for s in range(spans):
                here = slice(s * span, (s + 1) * span)
                x = x_ref[here, at].astype(jnp.float32)
                u = (step[here, at] * x).astype(jnp.bfloat16)
                out = k_ref[:, at] * x
                for j in range(2):
                    head = 2 * pair + j
                    gap = columns[here, head : head + 1] - g_ref[0, head : head + 1, here]
                    mixing = (jnp.exp(jnp.minimum(gap, 0.0)) * i_ref[s]).astype(jnp.bfloat16)
                    mine = (lane >= head_dim) if j else (lane < head_dim)
                    out += jnp.dot(
                        mixing,
                        jnp.where(mine, u, jnp.zeros_like(u)),
                        preferred_element_type=jnp.float32,
                    )
                if s:
                    out += grow[here, at] * jnp.dot(
                        c_ref[here, :], state.astype(jnp.bfloat16), preferred_element_type=jnp.float32
                    )
                if s + 1 < spans:
                    weighted = (u.astype(jnp.float32) * fade[here, at]).astype(jnp.bfloat16)
                    fresh = lax.dot_general(
                        b_ref[here, :],
                        weighted,
                        (((0,), (0,)), ((), ())),
                        preferred_element_type=jnp.float32,
                    )
                    last = grow[(s + 1) * span - 1 : (s + 1) * span, at]
                    state = fresh if state is None else last * state + fresh
                o_ref[here, at] = out

    full = lambda a: pl.BlockSpec(a.shape, lambda i: (0,) * a.ndim)
    return pl.pallas_call(
        kernel,
        grid=(count,),
        in_specs=[
            pl.BlockSpec((length, group), lambda i: (0, i + offset)),
            full(steps),
            full(fades),
            full(grown),
            pl.BlockSpec((1, heads, length), lambda i: (i + offset, 0, 0)),
            full(write_rows),
            full(read_rows),
            pl.BlockSpec((1, group), lambda i: (0, i + offset)),
        ]
        + [pl.BlockSpec(memory_space=pl.ANY)] * len(buffers),
        out_specs=pl.BlockSpec((length, group), lambda i: (0, i + offset)),
        out_shape=pltpu.HBM((length, channels), jnp.float32),
        scratch_shapes=[pltpu.VMEM((spans, span, span), jnp.float32)],
        input_output_aliases={8: 0} if buffers else {},
        cost_estimate=pl.CostEstimate(
            flops=2 * length * count * group * span * 2,
            transcendentals=length * span * count * heads,
            bytes_accessed=6 * length * count * group,
        ),
        compiler_params=pltpu.CompilerParams(vmem_limit_bytes=14 << 20),
        name="local_outputs",
    )(*held(inputs, steps, fades, grown, rows, write_rows, read_rows, skip, *buffers))


def partial_outputs(
    local, packed, read_rows, entering, gain, weight, head_dim, slots, heads, at, sizes
):
    length, channels = local.shape
    width = weight.shape[1]
    group = heads * head_dim
    tile = width // 4
    here = slice(at, at + sum(sizes))

    def kernel(y_ref, p_ref, c_ref, s_ref, g_ref, w_ref, *refs):
        o_refs, a_ref = refs[:-1], refs[-1]
        i = pl.program_id(0)
        row = lax.broadcasted_iota(jnp.int32, (group, group), 0)
        col = lax.broadcasted_iota(jnp.int32, (group, group), 1)
        same = (lax.bitwise_xor(row, col) < head_dim).astype(jnp.bfloat16)
        carried = lax.dot_general(
            c_ref[here, :], s_ref[...], (((1,), (1,)), ((), ())), preferred_element_type=jnp.float32
        )
        spread = expander(i * heads, 0, group, head_dim, slots)
        factor = jnp.dot(p_ref[here, :], spread, preferred_element_type=jnp.float32)
        y = y_ref[here, :] + carried * factor
        square = y * y
        high = square.astype(jnp.bfloat16)
        low = (square - high.astype(jnp.float32)).astype(jnp.bfloat16)
        sums = jnp.dot(high, same, preferred_element_type=jnp.float32) + jnp.dot(
            low, same, preferred_element_type=jnp.float32
        )
        y = (y * lax.rsqrt(sums / head_dim + EPSILON) * g_ref[...]).astype(jnp.bfloat16)

        @pl.when(i == 0)
        def _():
            a_ref[...] = jnp.zeros_like(a_ref)

        for t in range(0, width, tile):
            a_ref[:, t : t + tile] += jnp.dot(
                y, w_ref[:, t : t + tile], preferred_element_type=jnp.float32
            )

        @pl.when(i + 1 == pl.num_programs(0))
        def _():
            top = 0
            for o_ref in o_refs:
                o_ref[...] = a_ref[top : top + o_ref.shape[0], :].astype(o_ref.dtype)
                top += o_ref.shape[0]

    rows = sum(sizes)
    return pl.pallas_call(
        kernel,
        grid=(channels // group,),
        in_specs=[
            pl.BlockSpec((length, group), lambda i: (0, i)),
            pl.BlockSpec(packed.shape, lambda i: (0, 0)),
            pl.BlockSpec(read_rows.shape, lambda i: (0, 0)),
            pl.BlockSpec((group, read_rows.shape[1]), lambda i: (i, 0)),
            pl.BlockSpec((1, group), lambda i: (0, i)),
            pl.BlockSpec((group, width), lambda i: (i, 0)),
        ],
        out_specs=[pl.BlockSpec((n, width), lambda i: (0, 0)) for n in sizes],
        out_shape=[pltpu.HBM((n, width), jnp.bfloat16) for n in sizes],
        scratch_shapes=[pltpu.VMEM((rows, width), jnp.float32)],
        cost_estimate=pl.CostEstimate(
            flops=2 * rows * channels * width,
            transcendentals=rows * channels,
            bytes_accessed=2 * width * channels,
        ),
        compiler_params=pltpu.CompilerParams(vmem_limit_bytes=23 << 20),
        name="partial_outputs",
    )(*held(local, packed, read_rows), entering, gain, weight)


def flip(x, bit):
    size = lax.axis_size("seq")
    return lax.ppermute(x, "seq", [(i, i ^ bit) for i in range(size)])


def shift(x, by):
    size = lax.axis_size("seq")
    return lax.ppermute(x, "seq", [(i, i + by) for i in range(size - by)])


def swap(x):
    return lax.ppermute(x, "tp", [(0, 1), (1, 0)])


def pack(state, decay):
    high = decay.astype(jnp.bfloat16)
    low = (decay - high.astype(jnp.float32)).astype(jnp.bfloat16)
    size = state.shape[2]
    return jnp.concatenate(
        [state.astype(jnp.bfloat16).reshape(-1, size), high.reshape(-1, size), low.reshape(-1, size)]
    )


def unpack(rows, heads):
    size = rows.shape[1]
    at = rows.shape[0] - 2 * heads
    state = rows[:at].astype(jnp.float32).reshape(heads, -1, size)
    tail = rows[at:].astype(jnp.float32)
    return state, (tail[:heads] + tail[heads:]).reshape(heads, 1, size)


def entering_state(rows, heads):
    place = lax.axis_index("seq")
    planes = lax.axis_size("seq") // 4
    core = place % 2
    side = place // 2 % 2
    half, quarter = heads // 2, heads // 4

    def part(pair, index, size):
        return tuple(lax.dynamic_slice_in_dim(a, index * size, size, 0) for a in pair)

    def ordered(mine, other, bit):
        first = jax.tree.map(lambda a, b: jnp.where(bit == 0, a, b), mine, other)
        second = jax.tree.map(lambda a, b: jnp.where(bit == 0, b, a), mine, other)
        return first, second

    def joined(first, second):
        return second[1] * first[0] + second[0], first[1] * second[1]

    mine = unpack(rows, heads)
    other = flip(rows, 1)
    other = unpack(other, heads)
    first, second = ordered(mine, other, core)
    chip = joined(part(first, core, half), part(second, core, half))
    chip_rows = pack(*chip)
    chip = unpack(chip_rows, half)
    other_chip = flip(chip_rows, 2)
    first_chip, second_chip = ordered(chip, unpack(other_chip, half), side)
    plane_rows = pack(*joined(part(first_chip, side, quarter), part(second_chip, side, quarter)))
    before = jnp.zeros((quarter,) + chip[0].shape[1:], jnp.float32)
    arrived = []
    for by in range(1, planes):
        arrived.append(shift(plane_rows, 4 * by))
    for state, decay in [unpack(a, quarter) for a in reversed(arrived)]:
        before = state + decay * before
    before = before.astype(jnp.bfloat16)

    def whole(own, bit, distance):
        got = flip(own, distance)
        return jnp.where(
            bit == 0, jnp.concatenate([own, got]), jnp.concatenate([got, own])
        ).astype(jnp.float32)

    before = whole(before, side, 2)
    before = jnp.where(side == 1, first_chip[1] * before + first_chip[0], before)
    before = whole(before.astype(jnp.bfloat16), core, 1)
    return jnp.where(core == 1, first[1] * before + first[0], before).astype(jnp.bfloat16)


def on_device(
    mixer_input, state_write, state_read, step_size, log_decay, skip_gain, head_gain,
    mixer_out, residual, attn_gain, qkv_weight,
):
    tokens, channels = mixer_input.shape
    head_count = step_size.shape[1]
    head_dim = channels // head_count
    span_len = min(tokens, 256)
    spans = tokens // span_len
    slots = 32
    heads = 4
    side = lax.axis_index("tp")
    far_residual = swap(residual)

    payload, steps, fades, carries, gaps, rows = write_states(
        mixer_input, step_size.T, log_decay.T, state_write, head_dim, slots, heads, spans
    )
    rows = rows.reshape(head_count // heads, heads, tokens)
    size = payload.shape[1]
    local, offset = [], 0
    for count in LOCAL:
        count = head_count // heads * count // sum(LOCAL)
        local = [
            local_outputs(
                mixer_input, steps, fades, gaps, rows, state_write, state_read,
                jnp.repeat(skip_gain, head_dim)[None], head_dim, slots, heads, spans,
                offset, count, local,
            )
        ]
        offset += count
    entering = entering_state(payload, head_count).reshape(channels, size)

    weight = jnp.transpose(qkv_weight, (1, 0, 2))
    place = lax.axis_index("seq")
    core = place % 2
    plane_side = place // 2 % 2
    sizes = [tokens * count // sum(CHUNKS) for count in CHUNKS]
    owns, done = [], 0
    for some in (sizes[:1], sizes[1:]):
        owns += partial_outputs(
            local[0], carries, state_read, entering, head_gain[None], mixer_out, head_dim,
            slots, heads, done, some,
        )
        done += sum(some)
    at, buffers, kept = 0, [], [[], [], [], [], []]
    for k, count in enumerate(CHUNKS):
        rows = tokens * count // sum(CHUNKS)
        own = owns[k]
        got = swap(own)
        *buffers, mine = stream_and_project(
            own, got, residual, far_residual, side[None], attn_gain[None], weight, at, buffers
        )
        far = shift(mine, 4)
        near = flip(jnp.where(core == 0, mine, far), 1)
        across = flip(jnp.where(plane_side == 0, mine, far), 2)
        corner = flip(across, 1)
        for held, piece in zip(kept, (far, near, across, corner, mine)):
            held.append(piece)
        at += rows
    streams, normed_stream = buffers
    queries = project_queries(normed_stream, weight)
    back = jnp.stack(
        [4 + 0 * core, jnp.where(core == 1, 1, 3), 2 + 0 * core, jnp.where(core == 1, 3, 1)]
    )
    valid = (place >= back).astype(jnp.int32)
    attended = attend(queries, kept, valid, AHD)
    return streams, attended


def solution(mesh):
    placed = (
        P("seq", "tp"), P("seq", None), P("seq", None), P("seq", "tp"), P("seq", "tp"),
        P("tp"), P("tp"), P("tp", None), P("seq", "tp"), P(), P(None, None, "tp"),
    )

    return jax.shard_map(
        on_device, mesh=mesh, in_specs=placed, out_specs=(P("seq", "tp"), P("seq", "tp")),
        check_vma=False,
    )
```
